32 devices in a mesh: dp: 4 (over y, x), expert: 8 (over z, core).
Axes of the slice: x: 2, y: 2, z: 4, core: 2. Of those that a mesh axis runs over, the one named last changes fastest.
Arguments:
- tokens: bfloat16 [256, 4096], P(('dp', 'expert')), may hold values from -6 to 6
- route_weight: float32 [256, 8], P(('dp', 'expert')), may hold values from 0.1 to 1
- expert_ids: int32 [256, 8], P(('dp', 'expert')), may hold values from 0 to 15, all different within a row; in each aligned block of 8 rows (0 to 7, 8 to 15, ...) at most 8 rows name the same one
- placement: int32 [16], replicated, may hold values from 0 to 15, each once
- pair_step: int32 [8], replicated, may hold values from 0 to 1
- move_slot: int32 [8], replicated, may hold values from 0 to 1
- expert_weights: bfloat16 [16, 3, 4096, 1024], P('expert', None, None, 'dp'), may hold values from -0.375 to 0.375
Outputs:
- mixed: bfloat16 [256, 4096], P(('dp', 'expert'))
- moved_weights: bfloat16 [8, 3, 4096, 1024], P('expert', None, None, 'dp')
The draws below stay inside these ranges and needn't reach their ends.
Inputs may be any that keep to these rules, and one draw needn't show every extreme that they name: `expert_ids`: each row names 8 different experts. Among the rows of one device (aligned blocks of 8 rows, in the order of the tokens) no expert is named more than 8 times, a bound that some block reaches. A permutation of the slots: expert x is held in slot placement[x], which belongs to index placement[x] // 2 of expert.
All inputs are finite; a program needn't handle non-finite values.
Results may differ from the reference program's by a relative error of at most 0.012.
Values may be sent and summed in bfloat16 or wider, within the bound.
A program may use at most 128 MiB of HBM per device.

```python
import math
import jax
import jax.numpy as jnp
import numpy as np
from jax import lax

D = 4096
FF = 1024
TOP = 8
EXP_COL = 2
TOK_DEV = 8
EXPERTS = 16
CAP = 8
TOKENS = 256
N_DP = 4
N_EXPERT = 8


def place_ends(drawn, own_key, least, top_value):
    index_at = [jax.random.randint(jax.random.fold_in(own_key, axis), (), 0, length) for axis, length in enumerate(drawn.shape)]
    longest = drawn.shape.index(max(drawn.shape))
    beside = index_at[:longest] + [(index_at[longest] + 1) % drawn.shape[longest]] + index_at[longest + 1:]
    return drawn.at[tuple(index_at)].set(least).at[tuple(beside)].set(top_value)


def block_scale(key, dims, shards, least, top_value):
    def one(dim, blocks):
        draws = jax.random.uniform(jax.random.fold_in(jax.random.fold_in(key, 6), dim), (blocks,), jnp.float32, least / len(shards), top_value / len(shards))
        return jnp.repeat(jnp.exp(draws), dims[dim] // blocks).reshape((-1,) + (1,) * (len(dims) - dim - 1))

    factor_of = one(*shards[0])
    for cut in shards[1:]:
        factor_of = factor_of * one(*cut)
    return factor_of


def assign_block(rng, own, number, rows, count, top, reach, lean):
    sequence = jax.random.permutation(rng, count)
    heavy_load, ordinary = shares(count, rows * top, reach, lean, True), shares(count, rows * top, reach, lean, False)
    places = jnp.arange(count)

    def named(lengths, rotation):
        used = int((lengths > 0).sum())
        fixed = max(1, used // 4)
        shifted = fixed + (places - fixed + rotation * (used - fixed)) % max(1, count - fixed)
        return jnp.zeros((count,), jnp.int32).at[sequence[jnp.where(places < fixed, places, shifted)]].set(jnp.asarray(lengths, jnp.int32))

    lengths = jnp.where(number % 4 == 0, named(heavy_load, number // 4), named(ordinary, number - number // 4 - 1))
    mixed = jax.random.permutation(jax.random.fold_in(own, 3), count)
    source_of, receiver = mixed[0:count // 2 * 2:2], mixed[1:count // 2 * 2:2]
    margin = jnp.minimum(lengths[source_of] - 1, reach - lengths[receiver]) // 2
    margin = jnp.where((source_of == sequence[0]) | (receiver == sequence[0]) | (lengths[receiver] == 0), 0, jnp.maximum(margin, 0))
    shifted = jax.random.randint(jax.random.fold_in(own, 4), (count // 2,), 0, 1 << 20) % (margin + 1)
    lengths = lengths.at[source_of].add(-shifted).at[receiver].add(shifted)
    members = jnp.searchsorted(jnp.cumsum(lengths), jnp.arange(rows * top), side="right").astype(jnp.int32)
    grid = members.reshape(top, rows).T
    grid = grid[jax.random.permutation(jax.random.fold_in(own, 1), rows)]
    rotation = jax.random.randint(jax.random.fold_in(own, 2), (rows, 1), 0, top)
    return jnp.take_along_axis(grid, (jnp.arange(top)[None, :] + rotation) % top, axis=1)


def shares(number_of, total, bound, lean, full):
    loads = [(1 << 20) // math.isqrt(grade ** lean) + 1 for grade in range(1, number_of + 1)]
    largest = bound if full else min(bound, max(-(-total // number_of), total * loads[0] // sum(loads)))
    least = 1 if total - largest >= number_of - 1 else 0
    given, rest = [largest] + [least] * (number_of - 1), total - largest - least * (number_of - 1)
    while rest > 0:
        candidates = [i for i in range(1, number_of) if given[i] < largest] or [i for i in range(1, number_of) if given[i] < bound]
        whole, left = sum([loads[i] for i in candidates]), rest
        for i in candidates:
            more = min(bound - given[i], max(1, left * loads[i] // whole), rest)
            given[i] = given[i] + more
            rest = rest - more
    return np.array(given)


def normal_values(key, dims, deviation, most, split=(), held_as=jnp.bfloat16):
    array = deviation * jax.random.normal(key, dims, jnp.float32)
    if split:
        array = array * block_scale(key, dims, split, -0.22, 0.18)
    return jnp.clip(array, -most, most).astype(held_as)


def setup_inputs(seed: int = 0) -> dict:
    keys = jax.random.split(jax.random.key(seed), 8)
    tokens = normal_values(keys[0], (TOKENS, D), 1.0, 6.0, ((0, 32),))
    route_weight = jnp.clip(0.1 + 0.9 * jax.random.uniform(keys[1], (TOKENS, TOP), jnp.float32) ** block_scale(keys[1], (TOKENS, TOP), ((0, 32),), -0.2, 0.2), 0.1, 1.0)
    expert_ids_keys = jax.random.split(jax.random.fold_in(keys[2], 1), TOKENS // TOK_DEV)
    expert_ids_turns = jax.random.permutation(jax.random.fold_in(keys[2], 3), TOKENS // TOK_DEV)
    expert_ids = jax.vmap(lambda own, number: assign_block(jax.random.fold_in(keys[2], 2), own, number, TOK_DEV, EXPERTS, TOP, CAP, 2))(expert_ids_keys, expert_ids_turns).reshape((TOKENS, TOP))
    placement = jax.random.permutation(keys[3], EXPERTS).astype(jnp.int32)
    pair_step = place_ends(jax.random.randint(keys[4], (N_EXPERT,), 0, 2), jax.random.fold_in(keys[4], 1), 0, 1).astype(jnp.int32)
    move_slot = place_ends(jax.random.randint(keys[5], (N_EXPERT,), 0, EXP_COL), jax.random.fold_in(keys[5], 1), 0, EXP_COL - 1).astype(jnp.int32)
    expert_weights = normal_values(keys[6], (EXPERTS, 3, D, FF), (1.5 * D ** -0.5), 0.375, ((0, 8), (3, 4)))
    return dict(tokens=tokens, route_weight=route_weight, expert_ids=expert_ids, placement=placement, pair_step=pair_step, move_slot=move_slot, expert_weights=expert_weights)


def pair_offsets(flags):
    count = flags.shape[0]
    columns = jnp.arange(count, dtype=jnp.int32)
    joined = jnp.repeat(jnp.sum(flags.reshape(-1, 2), axis=1) > 0, 2)
    return jnp.where(joined, 1 - 2 * (columns % 2), 0).astype(jnp.int32)


def reference(tokens, route_weight, expert_ids, placement, pair_step, move_slot, expert_weights):
    columns = jnp.arange(N_EXPERT, dtype=jnp.int32)
    source = (columns + pair_offsets(pair_step)).astype(jnp.int32)
    src_slot = (source * EXP_COL + move_slot[source]).astype(jnp.int32)
    moved_weights = expert_weights[src_slot]
    flat_ids = expert_ids.reshape(-1).astype(jnp.int32)
    matches = (flat_ids[:, None] == jnp.arange(EXPERTS, dtype=jnp.int32)[None, :]).astype(jnp.int32)
    position = jnp.sum(matches * (jnp.cumsum(matches, axis=0) - 1), axis=1).astype(jnp.int32)
    rows_per = (TOKENS // TOK_DEV) * CAP
    token_of = jnp.arange(TOKENS * TOP, dtype=jnp.int32) // TOP
    buffer = jnp.zeros((EXPERTS, rows_per, D), jnp.bfloat16).at[flat_ids, position].set(tokens[token_of])

    def one_expert(pair_in):
        row_data, expert_index = pair_in
        weights = lax.dynamic_index_in_dim(expert_weights, placement[expert_index], 0, keepdims=False)
        gate_act = jnp.dot(row_data, weights[0], preferred_element_type=jnp.float32)
        up_act = jnp.dot(row_data, weights[1], preferred_element_type=jnp.float32)
        hidden = (jax.nn.silu(gate_act) * up_act).astype(jnp.bfloat16)
        grouped = hidden.reshape(rows_per, N_DP, FF // N_DP).astype(jnp.float32)
        down_weight = weights[2].reshape(D, N_DP, FF // N_DP).astype(jnp.float32)
        partial_value = jnp.einsum("rgh,dgh->rgd", grouped, down_weight).astype(jnp.bfloat16)
        partial_value = lax.optimization_barrier(partial_value).astype(jnp.float32)
        return jnp.sum(partial_value, axis=1).astype(jnp.bfloat16)

    outputs = lax.map(one_expert, (buffer, jnp.arange(EXPERTS, dtype=jnp.int32)))
    picked = outputs[flat_ids, position].reshape(TOKENS, TOP, D).astype(jnp.float32)
    mixed = jnp.sum(route_weight[:, :, None] * picked, axis=1).astype(jnp.bfloat16)
    return mixed, moved_weights
```

```python
import functools

import jax
import jax.numpy as jnp
from jax import lax
from jax.experimental import pallas as pl
from jax.experimental.pallas import tpu as pltpu
from jax.sharding import PartitionSpec as P

MESH = pl.DeviceIdType.MESH
LANES = 128
VMEM_LIMIT = 60 * 1024 * 1024
F32, BF16 = jnp.float32, jnp.bfloat16


def visit(nz):
    order = [0]
    for i in range(1, nz // 2 + 1):
        order += [i] if i == nz - i else [i, nz - i]
    return order[:nz]


def layer_kernel(
    nd, nz, place_ref, mv_ref, x_ref, rw_ref, id_ref, w_hbm, y_ref, own_ref, got_ref,
    g_ref, t_ref, h_ref, wt_ref, rc_ref, rx1_ref, ry1_ref, rx2_ref, ry2_ref, ra_ref, *rest,
):
    d = lax.axis_index("dp")
    e = lax.axis_index("expert")
    zz, c = e // 2, e % 2
    ny = nd // 2
    y, x = d // 2, d % 2
    other = 1 - x
    slots, parts, width, hidden = w_hbm.shape
    w_refs = rest[:parts]
    (w_sem, s_send, s_recv, z_send, z_recv, bx_send, bx_recv, by_send, by_recv,
     d1_send, d1_recv, d2_send, d2_recv, c_send, c_recv, rc_send, rc_recv,
     rx1_send, rx1_recv, ry1_send, ry1_recv, rx2_send, rx2_recv, ry2_send, ry2_recv,
     ra_send, ra_recv) = rest[parts:]
    tokens = x_ref.shape[0]
    lanes = g_ref.shape[5] - width
    half = width // 2
    lo, hi = pl.ds(0, half), pl.ds(half, half)
    order = visit(nz)
    experts = place_ref.shape[0]

    loads = [
        [pltpu.make_async_copy(w_hbm.at[j, m], w_refs[m].at[j], w_sem.at[j, m]) for j in range(slots)]
        for m in range(parts)
    ]
    for part in loads:
        for load in part:
            load.start()

    lane = lax.broadcasted_iota(jnp.int32, (tokens, lanes), 1)
    name = jnp.where(lane < experts, lane, jnp.where(lane < 2 * experts, lane - experts, -1))
    share = jnp.zeros(lane.shape, F32)
    for k in range(id_ref.shape[1]):
        share += jnp.where(name == id_ref[:, k : k + 1], rw_ref[:, k : k + 1], 0.0)
    high = share.astype(BF16).astype(F32)
    g_ref[c, 0, y, x, :, :width] = x_ref[...]
    g_ref[c, 0, y, x, :, width:] = jnp.where(lane < experts, high, share - high).astype(BF16)

    sibling = {"dp": d, "expert": zz * 2 + 1 - c}
    beside = {"dp": y * 2 + other, "expert": e}

    def along_y(k):
        return {"dp": lax.rem(y + k, ny) * 2 + x, "expert": e}

    def ahead(i):
        return {"dp": d, "expert": lax.rem(zz + i, nz) * 2 + c}

    def back_y(k):
        return lax.rem(y - k + ny, ny)

    barrier = pltpu.get_barrier_semaphore()
    peers = [sibling, beside] + [along_y(k) for k in range(1, ny)] + [ahead(i) for i in range(1, nz)]
    for peer in peers:
        pl.semaphore_signal(barrier, inc=1, device_id=peer, device_id_type=MESH)
    pl.semaphore_wait(barrier, len(peers))

    sent = []

    def send(src, dst, send_sem, recv_sem, peer, keep=None):
        copy = pltpu.make_async_remote_copy(
            src_ref=src, dst_ref=dst, send_sem=send_sem, recv_sem=recv_sem,
            device_id=peer, device_id_type=MESH,
        )
        copy.start()
        (sent if keep is None else keep).append(copy)

    def arrived(dst, recv_sem):
        pltpu.make_async_remote_copy(
            src_ref=dst, dst_ref=dst, send_sem=recv_sem, recv_sem=recv_sem,
            device_id=sibling, device_id_type=MESH,
        ).wait_recv()

    gathers = [[] for _ in range(nz)]
    wide = [pl.ds(0, half), pl.ds(half, width + lanes - half)]

    def to_core(k, n, yy, xx):
        block = g_ref.at[c, k, yy, xx]
        send(block, block, c_send.at[k, n], c_recv.at[k, n], sibling, gathers[k])

    def spread(k):
        block = g_ref.at[c, k, y, x]
        if k:
            arrived(block, z_recv.at[k - 1])
        send(block, block, bx_send.at[k], bx_recv.at[k], beside, gathers[k])
        for i in range(1, ny):
            send(block, block, by_send.at[k, i - 1], by_recv.at[k, i - 1], along_y(i), gathers[k])
        to_core(k, 0, y, x)

    def forward(k):
        arrived(g_ref.at[c, k, y, other], bx_recv.at[k])
        block = g_ref.at[c, k, y, other, :, wide[0]]
        for i in range(1, ny):
            send(block, block, d1_send.at[k, i - 1], d1_recv.at[k, i - 1], along_y(i), gathers[k])
        for i in range(1, ny):
            arrived(g_ref.at[c, k, back_y(i), x], by_recv.at[k, i - 1])
            block = g_ref.at[c, k, back_y(i), x, :, wide[1]]
            send(block, block, d2_send.at[k, i - 1], d2_recv.at[k, i - 1], beside, gathers[k])
        to_core(k, 1, y, other)
        for i in range(1, ny):
            to_core(k, 1 + i, back_y(i), x)

    def corner(k):
        for i in range(1, ny):
            arrived(g_ref.at[c, k, back_y(i), other, :, wide[0]], d1_recv.at[k, i - 1])
            arrived(g_ref.at[c, k, back_y(i), other, :, wide[1]], d2_recv.at[k, i - 1])
            to_core(k, ny + i, back_y(i), other)

    def from_core(k):
        arrived(g_ref.at[1 - c, k, y, x], c_recv.at[k, 0])
        arrived(g_ref.at[1 - c, k, y, other], c_recv.at[k, 1])
        for i in range(1, ny):
            arrived(g_ref.at[1 - c, k, back_y(i), x], c_recv.at[k, 1 + i])
            arrived(g_ref.at[1 - c, k, back_y(i), other], c_recv.at[k, ny + i])

    own = g_ref.at[c, 0, y, x]
    for k in range(1, nz):
        send(own, g_ref.at[c, k, y, x], z_send.at[k - 1], z_recv.at[k - 1], ahead(order[k]), gathers[0])
    spread(0)

    moving = mv_ref[e]
    tall = min(width, 256)

    def extract(m):
        for load in loads[m]:
            load.wait()

        def step(r, carry):
            at = pl.ds(pl.multiple_of(r * tall, tall), tall)
            own_ref[m, at, :] = w_refs[m][moving, at, :]
            return carry

        lax.fori_loop(0, width // tall, step, 0)

    def swap(m, n):
        at = pl.ds(n * half, half)
        send(own_ref.at[m, at], got_ref.at[m, at], s_send.at[m, n], s_recv.at[m, n], sibling)

    def turn():
        for j in range(slots):
            for q in range(0, width, 256):
                wt_ref[j * hidden : (j + 1) * hidden, q : q + 256] = w_refs[2][j, q : q + 256, :].T

    per_line = nd * tokens
    lines = h_ref.shape[0] // (2 * per_line)
    rows = lines * per_line
    row = lax.broadcasted_iota(jnp.int32, (1, lanes), 1)
    held = jnp.full((1, lanes), -1, jnp.int32)
    for n in range(experts):
        held = jnp.where((row == n) | (row == n + experts), place_ref[n], held)
    chunk = min(width, 1024)

    def gate_up(j, k0):
        at = pl.ds(k0, lines)
        if j == 0:
            for s in range(2):
                t_ref[s * rows : (s + 1) * rows, :] = (
                    g_ref[s, at, :, :, :, :width].astype(F32).reshape(rows, width).astype(BF16)
                )
        part = jnp.concatenate(
            [g_ref[s, at, :, :, :, width:].astype(F32).reshape(rows, lanes) for s in range(2)], axis=0
        )
        weight = jnp.sum(jnp.where(held == e * slots + j, part, 0.0), axis=1, keepdims=True)
        gate = jnp.zeros((2 * rows, hidden), F32)
        up = jnp.zeros((2 * rows, hidden), F32)
        for q in range(0, width, chunk):
            rows_in = t_ref[:, q : q + chunk]
            gate += jnp.dot(rows_in, w_refs[0][j, q : q + chunk, :], preferred_element_type=F32)
            up += jnp.dot(rows_in, w_refs[1][j, q : q + chunk, :], preferred_element_type=F32)
        value = weight * (gate / (1.0 + jnp.exp(-gate)) * up)
        h_ref[:, j * hidden : (j + 1) * hidden] = value.astype(BF16)

    def down(k0, side):
        at = pl.ds(k0, lines)
        for q in range(side * half, (side + 1) * half, chunk):
            total = jnp.dot(h_ref[...], wt_ref[:, q : q + chunk], preferred_element_type=F32)
            for s in range(2):
                g_ref[s, at, :, :, :, q : q + chunk] = (
                    total[s * rows : (s + 1) * rows].reshape(lines, ny, 2, tokens, chunk).astype(BF16)
                )

    each = nz // 2
    tiles = each // lines

    def to_sum(p, side):
        at, cols = pl.ds(p * each, each), (lo, hi)[side]
        send(
            g_ref.at[1 - c, at, :, :, :, cols], rc_ref.at[at, :, :, :, cols],
            rc_send.at[p, side], rc_recv.at[p, side], sibling,
        )

    def experts_of(p, between):
        if tiles == 1:
            k0 = p * each
            gate_up(0, k0)
            between[0]()
            for j in range(1, slots):
                gate_up(j, k0)
            between[1]()
            done(p)
            for side in range(2):
                down(k0, side)
                to_sum(p, side)
            return
        done(p)

        def step(n, carry):
            k0 = p * each + n * lines
            for j in range(slots):
                gate_up(j, k0)
            for side in range(2):
                down(k0, side)
            return carry

        lax.fori_loop(0, tiles, step, 0)
        for side in range(2):
            to_sum(p, side)
        between[0]()
        between[1]()

    def done(p):
        for k in range(p * each, (p + 1) * each):
            for copy in gathers[k]:
                copy.wait_send()

    def add(ref, index, *others):
        total = ref[index].astype(F32)
        for value in others:
            total += value.astype(F32)
        ref[index] = total.astype(BF16)

    def over_core(p, slots_in):
        for side in range(2):
            at, cols = pl.ds(p * each, each), (lo, hi)[side]
            arrived(rc_ref.at[at, :, :, :, cols], rc_recv.at[p, side])
            for k in slots_in:
                add(rc_ref, (k, slice(None), slice(None), slice(None), cols), g_ref[c, k, :, :, :, cols])
                if side == 0:
                    send(rc_ref.at[k, :, other, :, lo], rx1_ref.at[k], rx1_send.at[k], rx1_recv.at[k], beside)
                else:
                    for i in range(1, ny):
                        send(
                            rc_ref.at[k, lax.rem(y + i, ny), :, :, hi], ry2_ref.at[k, i - 1],
                            ry2_send.at[k, i - 1], ry2_recv.at[k, i - 1], along_y(i),
                        )

    def second(k):
        arrived(rx1_ref.at[k], rx1_recv.at[k])
        for i in list(range(1, ny)) + [0]:
            yy = lax.rem(y + i, ny)
            add(rc_ref, (k, yy, x, slice(None), lo), rx1_ref[k, yy])
            if i:
                send(
                    rc_ref.at[k, yy, x, :, lo], ry1_ref.at[k, i - 1],
                    ry1_send.at[k, i - 1], ry1_recv.at[k, i - 1], along_y(i),
                )
        for i in range(1, ny):
            arrived(ry2_ref.at[k, i - 1], ry2_recv.at[k, i - 1])
        for xx in (other, x):
            add(rc_ref, (k, y, xx, slice(None), hi), *[ry2_ref[k, i - 1, xx] for i in range(1, ny)])
            if xx is other:
                send(rc_ref.at[k, y, other, :, hi], rx2_ref.at[k], rx2_send.at[k], rx2_recv.at[k], beside)

    def third(k):
        for i in range(1, ny):
            arrived(ry1_ref.at[k, i - 1], ry1_recv.at[k, i - 1])
        add(rc_ref, (k, y, x, slice(None), lo), *[ry1_ref[k, i - 1] for i in range(1, ny)])
        arrived(rx2_ref.at[k], rx2_recv.at[k])
        add(rc_ref, (k, y, x, slice(None), hi), rx2_ref[k])
        if k:
            send(rc_ref.at[k, y, x], ra_ref.at[k - 1], ra_send.at[k - 1], ra_recv.at[k - 1], ahead(nz - order[k]))

    extract(0)
    swap(0, 0)
    spread(1)
    forward(0)
    swap(0, 1)
    extract(1)
    for k in range(2, nz):
        spread(k)
        if k == 2:
            swap(1, 0)
        forward(k - 1)
        corner(k - 2)
        if k == 2:
            extract(2)
            turn()
    swap(1, 1)
    for k in range(each):
        from_core(k)

    def last_forward():
        forward(nz - 1)

    def nothing():
        pass

    experts_of(0, (last_forward, nothing))
    for k in range(nz - 2, nz):
        corner(k)
    first = list(range(each - 1, -1, -1))
    later = list(range(each, nz))
    over_core(0, first)
    swap(2, 0)
    for k in later:
        from_core(k)
    experts_of(1, (nothing, nothing))
    second(first[0])
    over_core(1, later)
    for k in first[1:]:
        second(k)
    for k in first:
        third(k)
    swap(2, 1)
    for k in later:
        second(k)
    for k in later:
        third(k)
    final = rc_ref[0, y, x].astype(F32)
    for k in range(1, nz):
        arrived(ra_ref.at[k - 1], ra_recv.at[k - 1])
        final += ra_ref[k - 1].astype(F32)
    y_ref[...] = final.astype(BF16)
    for m in range(parts):
        for n in range(2):
            at = pl.ds(n * half, half)
            arrived(got_ref.at[m, at], s_recv.at[m, n])
    for copy in sent:
        copy.wait_send()


def write_kernel(step_ref, y_in, own_ref, got_ref, y_out, moved_out, y_sem, m_sem):
    first = lax.axis_index("expert") // 2 * 2
    swapping = step_ref[first] + step_ref[first + 1] > 0
    parts = own_ref.shape[0]
    small = pltpu.make_async_copy(y_in, y_out, y_sem)
    small.start()

    def put(src):
        copies = [pltpu.make_async_copy(src.at[m], moved_out.at[0, m], m_sem.at[m]) for m in range(parts)]
        for copy in copies:
            copy.start()
        for copy in copies:
            copy.wait()

    @pl.when(swapping)
    def _():
        put(got_ref)

    @pl.when(jnp.logical_not(swapping))
    def _():
        put(own_ref)

    small.wait()


def body(tokens, route_weight, expert_ids, placement, pair_step, move_slot, expert_weights):
    nd = lax.axis_size("dp")
    nz = lax.axis_size("expert") // 2
    ny = nd // 2
    rows, width = tokens.shape
    slots, parts, _, hidden = expert_weights.shape
    vmem = pl.BlockSpec(memory_space=pltpu.VMEM)
    smem = pl.BlockSpec(memory_space=pltpu.SMEM)
    anywhere = pl.BlockSpec(memory_space=pl.ANY)
    dma = pltpu.SemaphoreType.DMA
    full = width + -(-2 * placement.shape[0] // LANES) * LANES
    half = width // 2
    tile = min(nz // 2, max(1, 128 // (2 * nd * rows))) * 2 * nd * rows
    out, own, got = pl.pallas_call(
        functools.partial(layer_kernel, nd, nz),
        out_shape=(
            pltpu.VMEM((rows, width), BF16),
            pltpu.VMEM((parts, width, hidden), BF16),
            pltpu.VMEM((parts, width, hidden), BF16),
        ),
        in_specs=[smem, smem, vmem, vmem, vmem, anywhere],
        out_specs=(vmem, vmem, vmem),
        scratch_shapes=[
            pltpu.VMEM((2, nz, ny, 2, rows, full), BF16),
            pltpu.VMEM((tile, width), BF16),
            pltpu.VMEM((tile, slots * hidden), BF16),
            pltpu.VMEM((slots * hidden, width), BF16),
            pltpu.VMEM((nz, ny, 2, rows, width), BF16),
            pltpu.VMEM((nz, ny, rows, half), BF16),
            pltpu.VMEM((nz, ny - 1, rows, half), BF16),
            pltpu.VMEM((nz, rows, half), BF16),
            pltpu.VMEM((nz, ny - 1, 2, rows, half), BF16),
            pltpu.VMEM((nz - 1, rows, width), BF16),
        ]
        + [pltpu.VMEM((slots, width, hidden), BF16)] * parts
        + [dma((slots, parts))] + [dma((parts, 2))] * 2
        + [dma((nz - 1,))] * 2 + [dma((nz,))] * 2 + [dma((nz, ny - 1))] * 2
        + [dma((nz, ny - 1))] * 4 + [dma((nz, nd))] * 2 + [dma((2, 2))] * 2
        + [dma((nz,))] * 2 + [dma((nz, ny - 1))] * 2 + [dma((nz,))] * 2 + [dma((nz, ny - 1))] * 2
        + [dma((nz - 1,))] * 2,
        compiler_params=pltpu.CompilerParams(
            collective_id=0,
            has_side_effects=True,
            vmem_limit_bytes=VMEM_LIMIT - 4 * parts * width * hidden,
        ),
        name="layer",
    )(placement, move_slot, tokens, route_weight, expert_ids, expert_weights)
    return pl.pallas_call(
        write_kernel,
        out_shape=(
            jax.ShapeDtypeStruct((rows, width), BF16),
            jax.ShapeDtypeStruct((1, parts, width, hidden), BF16),
        ),
        in_specs=[smem, anywhere, anywhere, anywhere],
        out_specs=(anywhere, anywhere),
        scratch_shapes=[dma, dma((parts,))],
        compiler_params=pltpu.CompilerParams(vmem_limit_bytes=4 * 1024 * 1024),
        name="write",
    )(pair_step, out, own, got)


def solution(mesh):
    in_specs = (
        P(("dp", "expert"), None),
        P(("dp", "expert"), None),
        P(("dp", "expert"), None),
        P(),
        P(),
        P(),
        P("expert", None, None, "dp"),
    )
    out_specs = (P(("dp", "expert"), None), P("expert", None, None, "dp"))
    return jax.shard_map(body, mesh=mesh, in_specs=in_specs, out_specs=out_specs, check_vma=False)
```
